32 devices in a mesh: scan: 16 (over z, x, core), dict: 2 (over y).
Axes of the slice: x: 2, y: 2, z: 4, core: 2. Of those that a mesh axis runs over, the one named last changes fastest.
Arguments:
- patterns: bfloat16 [3600, 16384], P(None, 'scan'), may hold values from -210 to 210
- dictionary: bfloat16 [3600, 8192], P(None, ('scan', 'dict')), may hold values from -70 to 70
- orientation_quats: bfloat16 [4, 8192], P(None, ('scan', 'dict')), may hold values from -1 to 1
- phase_id: int32 [8192], P(('scan', 'dict')), may hold values from 0 to 2, as said below
- valid_count: int32 [32], P(('scan', 'dict')), may hold values from 1 to 256
Outputs:
- mean_quat: float32 [4, 16384], P(None, 'scan')
- phase_prob: float32 [3, 16384], P(None, 'scan')
The draws below stay inside these ranges and needn't reach their ends.
Inputs may be any that keep to these rules, and one draw needn't show every extreme that they name: `phase_id`: constant within each tile of 256 slots.
All inputs are finite; a program needn't handle non-finite values.
Results may differ from the reference program's by a relative error of at most 0.0029.
Values may be sent and summed in bfloat16 or wider, within the bound.
A program may use at most 128 MiB of HBM per device.

```python
import math
import jax
import jax.numpy as jnp
from jax import lax

PIX = 3600
TILE = 256
REACH = 3
PAT_DEV = 1024
PATTERNS = 16384
ORI = 8192
N_SCAN = 16
N_DICT = 2


def tile_bases(key):
    tiles = ORI // TILE
    base_key = jax.random.fold_in(key, 107)
    bases = jnp.clip(jax.random.normal(base_key, (5, tiles, PIX), jnp.float32), -2.5, 2.5)
    phases = jax.random.uniform(jax.random.fold_in(key, 109), (2, tiles), jnp.float32, 0.0, 2.0 * math.pi)
    return (bases, phases)


def dictionary_columns(key, columns):
    base = jax.random.fold_in(key, 101)
    bases, phases = tile_bases(key)
    tile = columns // TILE
    slot = (columns % TILE).astype(jnp.float32)
    first_angle = 2.0 * math.pi / TILE * slot + phases[0][tile]
    second_angle = 4.0 * math.pi / TILE * slot + phases[1][tile]

    def one_column(column):
        column_key = jax.random.fold_in(base, column)
        first_key, second_key = jax.random.split(column_key)
        values = jnp.clip(jax.random.normal(first_key, (PIX,), jnp.float32), -2.5, 2.5)
        return (values, jax.random.uniform(second_key, (), jnp.float32, -1.0, 1.0))
    noise, offset = jax.vmap(one_column)(columns)
    values = bases[0][tile]
    values = values + jnp.cos(first_angle)[:, None] * bases[1][tile]
    values = values + jnp.sin(first_angle)[:, None] * bases[2][tile]
    values = values + jnp.cos(second_angle)[:, None] * bases[3][tile]
    values = values + jnp.sin(second_angle)[:, None] * bases[4][tile]
    values = values + 0.6 * noise
    values = values * (1.0 / 1.85) + offset[:, None]
    return values.T


def tile_valid(key):
    tiles = ORI // TILE
    first_key, second_key, third_key = jax.random.split(jax.random.fold_in(key, 201), 3)
    trimmed = jax.random.randint(first_key, (tiles,), 0, TILE)
    filled = jax.random.randint(second_key, (tiles,), 0, 4) == 0
    chosen = jax.random.randint(third_key, (), 0, tiles)
    filled = filled | (jnp.arange(tiles) == chosen)
    return jnp.where(filled, TILE, TILE - trimmed).astype(jnp.int32)


def draw_valid_count(key, part):
    return tile_valid(key)


def draw_phase_id(key, part):
    per_tile = jax.random.randint(jax.random.fold_in(key, 301), (ORI // TILE,), 0, 3)
    return jnp.repeat(per_tile, TILE).astype(jnp.int32)


def draw_dictionary(key, part):
    values = dictionary_columns(key, jnp.arange(ORI, dtype=jnp.int32))
    return values.astype(jnp.bfloat16)


def draw_patterns(key, part):
    scan_rows = PATTERNS // PAT_DEV
    row_tiles = ORI // (TILE * scan_rows)
    keys = jax.random.split(jax.random.fold_in(key, 401), 10)
    block = jnp.arange(PATTERNS, dtype=jnp.int32) // PAT_DEV
    valid = tile_valid(key)
    first_row = (block + jax.random.randint(keys[0], (PATTERNS,), -REACH, REACH + 1)) % scan_rows
    first_tile = first_row * row_tiles + jax.random.randint(keys[1], (PATTERNS,), 0, row_tiles)
    first_slot = jax.random.randint(keys[2], (PATTERNS,), 0, valid[first_tile])
    first_column = first_tile * TILE + first_slot
    second_row = (block + jax.random.randint(keys[3], (PATTERNS,), -REACH, REACH + 1)) % scan_rows
    second_tile = second_row * row_tiles + jax.random.randint(keys[4], (PATTERNS,), 0, row_tiles)
    second_column = second_tile * TILE + jax.random.randint(keys[5], (PATTERNS,), 0, TILE)
    first_weight = jax.random.uniform(keys[6], (PATTERNS,), jnp.float32, 0.5, 1.0)
    second_weight = jax.random.uniform(keys[7], (PATTERNS,), jnp.float32, 0.5, 1.0)
    noise = jnp.clip(jax.random.normal(keys[8], (PIX, PATTERNS), jnp.float32), -6.0, 6.0)
    offsets = jax.random.uniform(keys[9], (PATTERNS,), jnp.float32, -2.0, 2.0)
    values = first_weight[None, :] * dictionary_columns(key, first_column)
    values = values + second_weight[None, :] * dictionary_columns(key, second_column)
    values = values + noise
    values = values + offsets[None, :]
    return values.astype(jnp.bfloat16)


def shard_levels(own_key, dims, cuts, low, high):
    level = 1.0
    for axis_at, blocks in cuts:
        heights = jax.random.uniform(jax.random.fold_in(jax.random.fold_in(own_key, 6), axis_at), (blocks,), jnp.float32, low / len(cuts), high / len(cuts))
        level = level * jnp.repeat(jnp.exp(heights), dims[axis_at] // blocks).reshape((-1,) + (1,) * (len(dims) - 1 - axis_at))
    return level


def setup_inputs(seed: int = 0) -> dict:
    key_of = jax.random.split(jax.random.key(seed), 6)
    return {
        "patterns": draw_patterns(jax.random.fold_in(key_of[5], 71), 0),
        "dictionary": draw_dictionary(jax.random.fold_in(key_of[5], 71), 0),
        "orientation_quats": jnp.clip(jax.random.uniform(key_of[2], (4, ORI), jnp.float32, -1.0, 1.0) * shard_levels(key_of[2], (4, ORI), ((1, 32),), -0.4, 0.0), -1.0, 1.0).astype(jnp.bfloat16),
        "phase_id": draw_phase_id(jax.random.fold_in(key_of[5], 71), 0),
        "valid_count": draw_valid_count(jax.random.fold_in(key_of[5], 71), 0),
    }


EPS = 1e-05
SHARPNESS = 40.0

def unit_columns(values):
    widened = values.astype(jnp.float32)
    centred = widened - lax.optimization_barrier(jnp.mean(widened, axis=0, keepdims=True))
    mean_square = lax.optimization_barrier(jnp.mean(centred * centred, axis=0, keepdims=True))
    return (centred * lax.rsqrt((mean_square + EPS) * values.shape[0])).astype(jnp.bfloat16)

def contribute(unit_tile, table_rows, unit_pats):
    cosine = jnp.dot(unit_tile.T, unit_pats, preferred_element_type=jnp.float32)
    weights = jnp.exp(SHARPNESS * (cosine - 1.0)).astype(jnp.bfloat16)
    return jnp.dot(table_rows, weights, preferred_element_type=jnp.float32)

def reference(patterns, dictionary, orientation_quats, phase_id, valid_count):
    row_length = N_DICT * TILE
    dict_rows = jnp.moveaxis(dictionary.reshape(PIX, N_SCAN, row_length), 1, 0)
    unit_rows = lax.map(unit_columns, dict_rows)
    live_slots = (jnp.arange(ORI) % TILE < jnp.repeat(valid_count, TILE)).astype(jnp.float32)
    phase_rows = (phase_id[None, :] == jnp.arange(3)[:, None]).astype(jnp.float32)
    tile_table = jnp.concatenate([orientation_quats.astype(jnp.float32), phase_rows, jnp.ones((1, ORI), jnp.float32)], 0)
    tile_table = (tile_table * live_slots[None, :]).astype(jnp.bfloat16)
    table_blocks = jnp.moveaxis(tile_table.reshape(8, N_SCAN, row_length), 1, 0)
    pattern_blocks = jnp.moveaxis(patterns.reshape(PIX, N_SCAN, PAT_DEV), 1, 0)

    def one_block(block_index):
        unit_pats = unit_columns(pattern_blocks[block_index])
        running = jnp.zeros((8, PAT_DEV), jnp.float32)
        for row_offset in range(-REACH, REACH + 1):
            source = (block_index + row_offset) % N_SCAN
            running = running + contribute(unit_rows[source], table_blocks[source], unit_pats)
        return running
    totals = lax.map(one_block, jnp.arange(N_SCAN, dtype=jnp.int32))
    totals = jnp.moveaxis(totals, 0, 1).reshape(8, PATTERNS)
    denominator = totals[7:8]
    return (totals[0:4] / denominator, totals[4:7] / denominator)
```

```python
import functools

import jax
import jax.numpy as jnp
from jax import lax
from jax.experimental import pallas as pl
from jax.experimental.pallas import tpu as pltpu
from jax.sharding import PartitionSpec as P

REACH = 3
SLOTS = 2 * REACH + 1
EPS = 1e-05
SHARPNESS = 40.0
LAYER = 4
LATE = 3


def chunk_count(pixels):
    for count in (15, 9, 5, 3, 25, 16, 8, 4, 2):
        if pixels % (16 * count) == 0:
            return count
    return 1


def kernel(
    n, n_dict, chunks, group, tile_ref, pats_ref, quats_ref, phase_ref, valid_ref,
    quat_out, prob_out,
    buf, pats, meta, acc, sums, totals, psum, quats, phase, valid,
    gate, ssem, rsem, meta_ssem, meta_rsem, load_sem, sum_ssem, sum_rsem,
):
    pixels, slots = tile_ref.shape
    rows = pixels // chunks
    own = REACH
    me = lax.axis_index("scan")
    my_dict = lax.axis_index("dict")
    j = lax.rem(me, LAYER)
    sign = jnp.where(j < 2, 1, -1)
    role = jnp.where((j == 0) | (j == LAYER - 1), 0, 1)
    rho = 1 - 2 * role

    def at(offset):
        return lax.rem(me + offset + n, n)

    def chunk(i):
        return pl.ds(pl.multiple_of(i * rows, 16), rows)

    core = lax.rem(me, 2)
    partner = rho * sign
    across = 2 * sign
    beyond = -3 * partner

    def scan_device(offset):
        return {"scan": at(offset)}

    def dict_device(d):
        return {"dict": lax.rem(my_dict + d, n_dict)}

    loads = [
        pltpu.make_async_copy(src, dst, load_sem.at[k])
        for k, (src, dst) in enumerate(
            (
                (tile_ref, buf.at[own]),
                (quats_ref, quats),
                (phase_ref, phase),
                (valid_ref, valid),
                (pats_ref, pats),
            )
        )
    ]
    for load in loads[:4]:
        load.start()

    barrier = pltpu.get_barrier_semaphore()
    pl.semaphore_signal(barrier, inc=1, device_id=scan_device(partner))
    pl.semaphore_signal(barrier, inc=1, device_id=scan_device(beyond))

    @pl.when(core == 1)
    def _():
        pl.semaphore_signal(barrier, inc=1, device_id=scan_device(across))
        for d in range(1, n_dict):
            pl.semaphore_signal(barrier, inc=1, device_id=dict_device(d))


    @pl.when(core == 0)
    def _():
        pl.semaphore_wait(barrier, 2)

    @pl.when(core == 1)
    def _():
        pl.semaphore_wait(barrier, 2 + n_dict)

    core_own = (0, None, partner, -rho)
    x_own = (1, None, across, 2)
    z_own = (2, None, beyond, 3 * rho)
    relay = (3, 2 + role, (4 - 2 * role) * sign, role - 2)
    core_mid = (4, 2, partner, 2 - rho)
    core_far = (5, -2, partner, -3)
    core_near = (6, -1, partner, -2)

    def send(flow, i, early=False):
        number, source, offset, slot = flow
        src = buf.at[own if source is None else source + own, chunk(i)]
        if early:
            src = tile_ref.at[chunk(i)]
        return pltpu.make_async_remote_copy(
            src_ref=src,
            dst_ref=buf.at[slot + own, chunk(i)],
            send_sem=ssem.at[number],
            recv_sem=rsem.at[slot + own, i],
            device_id={"scan": at(offset)},
        )

    def sent(flow):
        pltpu.make_async_copy(tile_ref, buf.at[own], ssem.at[flow[0]]).wait()

    def arrive(slot, i):
        pltpu.make_async_copy(
            tile_ref.at[chunk(i)], buf.at[slot + own, chunk(i)], rsem.at[slot + own, i]
        ).wait()

    def send_meta(flow):
        number, source, offset, slot = flow
        return pltpu.make_async_remote_copy(
            src_ref=meta.at[own if source is None else source + own],
            dst_ref=meta.at[slot + own],
            send_sem=meta_ssem.at[number],
            recv_sem=meta_rsem.at[slot + own],
            device_id={"scan": at(offset)},
        )

    def meta_arrive(slot):
        pltpu.make_async_copy(
            meta.at[own], meta.at[slot + own], meta_rsem.at[slot + own]
        ).wait()

    ahead = chunks // 3
    edge = jnp.where(role == 0, jnp.where(j == 0, me + LAYER >= n, me < LAYER), False)
    late = jnp.where(edge, LATE, 0)

    @pl.loop(0, ahead)
    def _(i):
        send(z_own, i, True).start()

        @pl.when(core == 1)
        def _():
            send(x_own, i, True).start()

    loads[4].start()
    pl.semaphore_signal(gate.at[0], inc=1, device_id=scan_device(partner))

    @pl.when(core == 1)
    def _():
        pl.semaphore_signal(gate.at[1], inc=1, device_id=scan_device(across))
        for d in range(1, n_dict):
            pl.semaphore_signal(gate.at[2], inc=1, device_id=dict_device(d))
        pl.semaphore_wait(gate.at[1], 1)
        pl.semaphore_signal(gate.at[1], inc=1, device_id=scan_device(partner))

    @pl.when(core == 0)
    def _():
        pl.semaphore_wait(gate.at[1], 1)

        @pl.loop(0, ahead)
        def _(i):
            send(x_own, i, True).start()

    pl.semaphore_wait(gate.at[0], 1)

    for load in loads[:4]:
        load.wait()

    def column_sums(ref, pieces, term):
        size = pixels // pieces
        width = ref.shape[-1]

        def step(i, s):
            piece = ref[pl.ds(pl.multiple_of(i * size, 16), size), :].astype(jnp.float32)
            value = term(piece).reshape(size // 8, 8, width)
            return s + jnp.sum(value, axis=0)

        total = lax.fori_loop(0, pieces, step, jnp.zeros((8, width), jnp.float32))
        return jnp.sum(total, axis=0, keepdims=True)

    def column_stats(ref, pieces):
        mean = column_sums(ref, pieces, lambda x: x) / pixels
        mean_square = column_sums(ref, pieces, lambda x: (x - mean) * (x - mean)) / pixels
        return mean, lax.rsqrt((mean_square + EPS) * pixels)

    mean, scale = column_stats(buf.at[own], 15)
    live = (
        lax.broadcasted_iota(jnp.int32, (1, slots), 1) < valid[0, 0]
    ).astype(jnp.float32)
    meta[own, 0:4, :] = quats[...].astype(jnp.float32) * live
    for p in range(3):
        meta[own, 4 + p : 5 + p, :] = (phase[...] == p).astype(jnp.float32) * live
    meta[own, 7:8, :] = live
    meta[own, 8:9, :] = mean
    meta[own, 9:10, :] = scale
    meta[own, 10:16, :] = jnp.zeros((6, slots), jnp.float32)

    for flow in (z_own, x_own, core_own):
        send_meta(flow).start()

    @pl.loop(ahead, chunks)
    def _(i):
        @pl.when((role == 1) | (i < chunks - late))
        def _():
            send(z_own, i).start()

        send(x_own, i).start()

    @pl.loop(0, chunks)
    def _(i):
        send(core_own, i).start()

    loads[4].wait()
    p_mean, p_scale = column_stats(pats, 25)

    def unit_step(i, s):
        size = pixels // 25
        part = pl.ds(pl.multiple_of(i * size, 16), size)
        unit = ((pats[part, :].astype(jnp.float32) - p_mean) * p_scale).astype(jnp.bfloat16)
        pats[part, :] = unit
        value = unit.astype(jnp.float32).reshape(size // 8, 8, unit.shape[-1])
        return s + jnp.sum(value, axis=0)

    unit_sum = lax.fori_loop(
        0, 25, unit_step, jnp.zeros((8, pats.shape[-1]), jnp.float32)
    )
    psum[...] = jnp.sum(unit_sum, axis=0, keepdims=True)

    totals[...] = jnp.zeros_like(totals)

    def product(slot, part):
        return lax.dot_general(
            buf[slot + own, part, :], pats[part, :], (((0,), (0,)), ((), ())),
            preferred_element_type=jnp.float32,
        )

    def accumulate(which, slot, g):
        part = pl.ds(pl.multiple_of(g * (group * rows), 16), group * rows)

        @pl.when(g == 0)
        def _():
            acc[which] = product(slot, part)

        @pl.when(g > 0)
        def _():
            acc[which] += product(slot, part)

    def arrive_all(slot):
        @pl.loop(0, chunks)
        def _(i):
            arrive(slot, i)

        meta_arrive(slot)

    def finish(which, slot):
        columns = jnp.transpose(meta[slot + own])
        m = columns[:, 8:9]
        s = columns[:, 9:10]
        cosine = (acc[which] - m * psum[...]) * s
        weights = jnp.exp(SHARPNESS * (cosine - 1.0)).astype(jnp.bfloat16)
        table = meta[slot + own, 0:8, :].astype(jnp.bfloat16)
        totals[...] += jnp.dot(table, weights, preferred_element_type=jnp.float32)

    everything = pl.ds(0, pixels)
    acc[0] = product(0, everything)
    finish(0, 0)
    arrive_all(rho)
    acc[1] = product(rho, everything)
    finish(1, rho)

    z_slot = -3 * rho
    first = jnp.where(role == 0, 2, z_slot)
    second = jnp.where(role == 0, z_slot, 2)

    meta_arrive(first)
    send_meta(relay).start()

    @pl.when(role == 0)
    def _():
        send_meta(core_mid).start()

    @pl.loop(0, chunks // group)
    def _(g):
        @pl.loop(0, group)
        def _(c):
            i = g * group + c
            arrive(first, i)
            send(relay, i).start()

            @pl.when(role == 0)
            def _():
                send(core_mid, i).start()

            @pl.when((role == 0) & (i >= ahead) & (i < ahead + late))
            def _():
                send(z_own, chunks - late + i - ahead).start()

        accumulate(0, first, g)

    finish(0, first)

    meta_arrive(second)

    @pl.when(role == 1)
    def _():
        send_meta(core_mid).start()

    @pl.loop(0, chunks // group)
    def _(g):
        @pl.loop(0, group)
        def _(c):
            i = g * group + c
            arrive(second, i)

            @pl.when(role == 1)
            def _():
                send(core_mid, i).start()

        accumulate(1, second, g)

    finish(1, second)

    mid_slot = 2 + rho
    arrive_all(mid_slot)
    acc[0] = product(mid_slot, everything)
    finish(0, mid_slot)

    far_slot = -2 - role
    near_slot = -1 - role
    meta_arrive(far_slot)
    meta_arrive(near_slot)

    @pl.when(role == 0)
    def _():
        send_meta(core_far).start()
        send_meta(core_near).start()

    @pl.loop(0, chunks // group)
    def _(g):
        @pl.loop(0, group)
        def _(c):
            i = g * group + c
            arrive(near_slot, i)

            @pl.when(role == 0)
            def _():
                send(core_near, i).start()

            arrive(far_slot, i)

            @pl.when(role == 0)
            def _():
                send(core_far, i).start()

        accumulate(0, far_slot, g)
        accumulate(1, near_slot, g)

    finish(0, far_slot)
    finish(1, near_slot)

    @pl.when(core == 1)
    def _():
        pl.semaphore_wait(gate.at[2], n_dict - 1)
        pl.semaphore_signal(gate.at[2], inc=1, device_id=scan_device(partner))

    @pl.when(core == 0)
    def _():
        pl.semaphore_wait(gate.at[2], 1)

    sums[my_dict] = totals[...]

    def send_sum(d):
        return pltpu.make_async_remote_copy(
            src_ref=totals,
            dst_ref=sums.at[my_dict],
            send_sem=sum_ssem.at[d],
            recv_sem=sum_rsem.at[my_dict],
            device_id={"dict": lax.rem(my_dict + d, n_dict)},
        )

    for d in range(1, n_dict):
        send_sum(d).start()

    for flow in (x_own, z_own, core_own, relay, core_mid):
        sent(flow)
        send_meta(flow).wait_send()

    @pl.when(role == 0)
    def _():
        for flow in (core_far, core_near):
            sent(flow)
            send_meta(flow).wait_send()

    for d in range(1, n_dict):
        source = lax.rem(my_dict + d, n_dict)
        pltpu.make_async_copy(totals, sums.at[source], sum_rsem.at[source]).wait()
    whole = sums[0]
    for d in range(1, n_dict):
        whole = whole + sums[d]
    denominator = whole[7:8]
    quat_out[...] = whole[0:4] / denominator
    prob_out[...] = whole[4:7] / denominator
    for d in range(1, n_dict):
        send_sum(d).wait_send()


def solution(mesh):
    n = mesh.shape["scan"]
    n_dict = mesh.shape["dict"]

    def per_device(patterns, dictionary, orientation_quats, phase_id, valid_count):
        pixels, slots = dictionary.shape
        count = patterns.shape[1]
        chunks = chunk_count(pixels)
        vmem = pl.BlockSpec(memory_space=pltpu.VMEM)
        hbm = pl.BlockSpec(memory_space=pltpu.HBM)
        return pl.pallas_call(
            functools.partial(kernel, n, n_dict, chunks, 3 if chunks % 3 == 0 else 1),
            out_shape=(
                jax.ShapeDtypeStruct((4, count), jnp.float32),
                jax.ShapeDtypeStruct((3, count), jnp.float32),
            ),
            in_specs=[hbm] * 5,
            out_specs=(vmem, vmem),
            scratch_shapes=[
                pltpu.VMEM((SLOTS, pixels, slots), jnp.bfloat16),
                pltpu.VMEM((pixels, count), jnp.bfloat16),
                pltpu.VMEM((SLOTS, 16, slots), jnp.float32),
                pltpu.VMEM((2, slots, count), jnp.float32),
                pltpu.VMEM((n_dict, 8, count), jnp.float32),
                pltpu.VMEM((8, count), jnp.float32),
                pltpu.VMEM((1, count), jnp.float32),
                pltpu.VMEM((4, slots), jnp.bfloat16),
                pltpu.VMEM((1, slots), jnp.int32),
                pltpu.SMEM((1, 1), jnp.int32),
                pltpu.SemaphoreType.REGULAR((3,)),
                pltpu.SemaphoreType.DMA((7,)),
                pltpu.SemaphoreType.DMA((SLOTS, chunks)),
                pltpu.SemaphoreType.DMA((7,)),
                pltpu.SemaphoreType.DMA((SLOTS,)),
                pltpu.SemaphoreType.DMA((5,)),
                pltpu.SemaphoreType.DMA((n_dict,)),
                pltpu.SemaphoreType.DMA((n_dict,)),
            ],
            compiler_params=pltpu.CompilerParams(
                collective_id=0, has_side_effects=True, vmem_limit_bytes=62 * 2**20
            ),
        )(dictionary, patterns, orientation_quats, phase_id.reshape(1, slots), valid_count.reshape(1, 1))

    in_specs = (
        P(None, "scan"),
        P(None, ("scan", "dict")),
        P(None, ("scan", "dict")),
        P(("scan", "dict")),
        P(("scan", "dict")),
    )
    out_specs = (P(None, "scan"), P(None, "scan"))
    return jax.shard_map(
        per_device, mesh=mesh, in_specs=in_specs, out_specs=out_specs, check_vma=False
    )
```

```python
import functools

import jax
import jax.numpy as jnp
from jax import lax
from jax.experimental import pallas as pl
from jax.experimental.pallas import tpu as pltpu
from jax.sharding import PartitionSpec as P

REACH = 3
SLOTS = 2 * REACH + 1
EPS = 1e-05
SHARPNESS = 40.0
LAYER = 4


def chunk_count(pixels):
    for count in (15, 9, 5, 3, 25, 16, 8, 4, 2):
        if pixels % (16 * count) == 0:
            return count
    return 1


def kernel(
    n, n_dict, chunks, group, tile_ref, pats_ref, quats_ref, phase_ref, valid_ref,
    quat_out, prob_out,
    buf, pats, meta, acc, sums, totals, quats, phase, valid,
    gate, ssem, rsem, meta_ssem, meta_rsem, load_sem, tile_sem, pats_sem, sum_ssem, sum_rsem,
):
    pixels, slots = tile_ref.shape
    rows = pixels // chunks
    own = REACH
    me = lax.axis_index("scan")
    my_dict = lax.axis_index("dict")
    j = lax.rem(me, LAYER)
    sign = jnp.where(j < 2, 1, -1)
    role = jnp.where((j == 0) | (j == LAYER - 1), 0, 1)
    rho = 1 - 2 * role

    def at(offset):
        return lax.rem(me + offset + n, n)

    def chunk(i):
        return pl.ds(pl.multiple_of(i * rows, 16), rows)

    core = lax.rem(me, 2)
    partner = rho * sign
    across = 2 * sign
    beyond = -3 * partner

    def scan_device(offset):
        return {"scan": at(offset)}

    def dict_device(d):
        return {"dict": lax.rem(my_dict + d, n_dict)}

    splits = 5

    def piece_of(i):
        size = pixels // splits
        return pl.ds(pl.multiple_of(i * size, 16), size)

    def load_tile(i):
        return pltpu.make_async_copy(
            tile_ref.at[piece_of(i)], buf.at[own, piece_of(i)], tile_sem.at[i]
        )

    def load_pats(i):
        return pltpu.make_async_copy(
            pats_ref.at[piece_of(i)], pats.at[piece_of(i)], pats_sem.at[i]
        )

    @pl.loop(0, splits)
    def _(i):
        load_tile(i).start()

    loads = [
        pltpu.make_async_copy(src, dst, load_sem.at[k])
        for k, (src, dst) in enumerate(
            ((quats_ref, quats), (phase_ref, phase), (valid_ref, valid))
        )
    ]
    for load in loads:
        load.start()

    barrier = pltpu.get_barrier_semaphore()
    pl.semaphore_signal(barrier, inc=1, device_id=scan_device(partner))
    pl.semaphore_signal(barrier, inc=1, device_id=scan_device(beyond))

    @pl.when(core == 1)
    def _():
        pl.semaphore_signal(barrier, inc=1, device_id=scan_device(across))
        for d in range(1, n_dict):
            pl.semaphore_signal(barrier, inc=1, device_id=dict_device(d))


    def column_stats(ref, lanes, load):
        width = ref.shape[-1]
        size = pixels // splits
        load(0).wait()
        shift = ref[pl.ds(0, 1), :].astype(jnp.float32)

        def piece(i, carry):
            @pl.when(i > 0)
            def _():
                load(i).wait()

            def step(k, carry):
                first, second = carry
                start = pl.multiple_of(i * size + k * lanes * 3, 16)
                x = ref[pl.ds(start, lanes * 3), :].astype(jnp.float32) - shift
                first = first + jnp.sum(x.reshape(3, lanes, width), axis=0)
                second = second + jnp.sum((x * x).reshape(3, lanes, width), axis=0)
                return first, second

            return lax.fori_loop(0, size // (lanes * 3), step, carry)

        zero = jnp.zeros((lanes, width), jnp.float32)
        first, second = lax.fori_loop(0, splits, piece, (zero, zero))
        first = jnp.sum(first, axis=0, keepdims=True) / pixels
        second = jnp.sum(second, axis=0, keepdims=True) / pixels
        return first + shift, lax.rsqrt((second - first * first + EPS) * pixels)

    mean, scale = column_stats(buf.at[own], 48, load_tile)

    for load in loads:
        load.wait()

    live = (
        lax.broadcasted_iota(jnp.int32, (1, slots), 1) < valid[0, 0]
    ).astype(jnp.float32)
    meta[own, 0:4, :] = quats[...].astype(jnp.float32) * live
    for p in range(3):
        meta[own, 4 + p : 5 + p, :] = (phase[...] == p).astype(jnp.float32) * live
    meta[own, 7:8, :] = live
    @pl.when(core == 0)
    def _():
        pl.semaphore_wait(barrier, 2)

    @pl.when(core == 1)
    def _():
        pl.semaphore_wait(barrier, 2 + n_dict)

    core_own = (0, None, partner, -rho)
    x_own = (1, None, across, 2)
    z_own = (2, None, beyond, 3 * rho)
    relay = (3, 2 + role, (4 - 2 * role) * sign, role - 2)
    core_mid = (4, 2, partner, 2 - rho)
    core_far = (5, -2, partner, -3)
    core_near = (6, -1, partner, -2)

    def send(flow, i, part=None):
        number, source, offset, slot = flow
        part = chunk(i) if part is None else part
        return pltpu.make_async_remote_copy(
            src_ref=buf.at[own if source is None else source + own, part],
            dst_ref=buf.at[slot + own, part],
            send_sem=ssem.at[number],
            recv_sem=rsem.at[slot + own, i],
            device_id={"scan": at(offset)},
        )

    def sent(flow):
        pltpu.make_async_copy(tile_ref, buf.at[own], ssem.at[flow[0]]).wait()

    def arrive(slot, i, part=None):
        part = chunk(i) if part is None else part
        pltpu.make_async_copy(
            tile_ref.at[part], buf.at[slot + own, part], rsem.at[slot + own, i]
        ).wait()

    everything = pl.ds(0, pixels)

    def block(g):
        return pl.ds(pl.multiple_of(g * (group * rows), 16), group * rows)

    def send_meta(flow):
        number, source, offset, slot = flow
        return pltpu.make_async_remote_copy(
            src_ref=meta.at[own if source is None else source + own],
            dst_ref=meta.at[slot + own],
            send_sem=meta_ssem.at[number],
            recv_sem=meta_rsem.at[slot + own],
            device_id={"scan": at(offset)},
        )

    def meta_arrive(slot):
        pltpu.make_async_copy(
            meta.at[own], meta.at[slot + own], meta_rsem.at[slot + own]
        ).wait()

    edge = jnp.where(role == 0, jnp.where(j == 0, me + LAYER >= n, me < LAYER), False)
    last = chunks - jnp.where(edge, group, 0)
    ahead = chunks // 3

    pl.semaphore_signal(gate.at[0], inc=1, device_id=scan_device(partner))

    @pl.when(core == 1)
    def _():
        pl.semaphore_signal(gate.at[1], inc=1, device_id=scan_device(across))
        for d in range(1, n_dict):
            pl.semaphore_signal(gate.at[2], inc=1, device_id=dict_device(d))

    def send_own(i, lanes):
        own_chunk = (buf[own, chunk(i), :].astype(jnp.float32) - mean) * scale
        buf[own, chunk(i), :] = own_chunk.astype(jnp.bfloat16)

        @pl.when(i < last)
        def _():
            send(z_own, i).start()

        if lanes:
            send(x_own, i).start()

    begin = group

    send_meta(z_own).start()

    @pl.when(core == 1)
    def _():
        send_meta(x_own).start()

        @pl.loop(0, begin)
        def _(i):
            send_own(i, True)

        pl.semaphore_wait(gate.at[1], 1)
        pl.semaphore_signal(gate.at[1], inc=1, device_id=scan_device(partner))

    @pl.when(core == 0)
    def _():
        @pl.loop(0, begin)
        def _(i):
            send_own(i, False)

        pl.semaphore_wait(gate.at[1], 1)
        send_meta(x_own).start()

        @pl.loop(0, begin)
        def _(i):
            send(x_own, i).start()

    @pl.loop(0, splits)
    def _(i):
        load_pats(i).start()

    @pl.loop(begin, chunks)
    def _(i):
        send_own(i, True)

    pl.semaphore_wait(gate.at[0], 1)
    send(core_own, 0, everything).start()

    send_meta(core_own).start()

    p_mean, p_scale = column_stats(pats, 16, load_pats)

    @pl.loop(0, 25)
    def _(i):
        size = pixels // 25
        part = pl.ds(pl.multiple_of(i * size, 16), size)
        pats[part, :] = ((pats[part, :].astype(jnp.float32) - p_mean) * p_scale).astype(
            jnp.bfloat16
        )

    totals[...] = jnp.zeros_like(totals)

    def product(slot, part):
        return lax.dot_general(
            buf[slot + own, part, :], pats[part, :], (((0,), (0,)), ((), ())),
            preferred_element_type=jnp.float32,
        )

    def accumulate(which, slot, g):
        if isinstance(g, int):
            acc[which] += product(slot, block(g))
            return

        @pl.when(g == 0)
        def _():
            acc[which] = product(slot, block(g))

        @pl.when(g > 0)
        def _():
            acc[which] += product(slot, block(g))

    def finish(which, slot):
        weights = jnp.exp(SHARPNESS * (acc[which] - 1.0)).astype(jnp.bfloat16)
        table = meta[slot + own].astype(jnp.bfloat16)
        totals[...] += jnp.dot(table, weights, preferred_element_type=jnp.float32)

    acc[0] = product(0, everything)
    finish(0, 0)
    arrive(rho, 0, everything)
    meta_arrive(rho)
    acc[1] = product(rho, everything)
    finish(1, rho)

    z_slot = -3 * rho
    mid_slot = 2 + rho
    far_slot = -2 - role
    near_slot = -1 - role
    groups = chunks // group

    def pieces(g, body):
        @pl.loop(0, group)
        def _(c):
            body(g * group + c)

    @pl.when(role == 0)
    def _():
        meta_arrive(2)
        send_meta(relay).start()
        send_meta(core_mid).start()

        @pl.loop(0, groups)
        def _(g):
            def step(i):
                arrive(2, i)
                send(relay, i).start()

                @pl.when((i >= ahead) & (last + i - ahead < chunks))
                def _():
                    send(z_own, last + i - ahead).start()

            pieces(g, step)
            send(core_mid, g, block(g)).start()
            accumulate(0, 2, g)

        finish(0, 2)
        meta_arrive(z_slot)

    @pl.when(role == 1)
    def _():
        meta_arrive(z_slot)
        send_meta(relay).start()

        @pl.loop(0, groups - 1)
        def _(g):
            def step(i):
                arrive(z_slot, i)
                send(relay, i).start()

            pieces(g, step)
            accumulate(2, z_slot, g)

        meta_arrive(2)
        send_meta(core_mid).start()

        @pl.loop(0, groups)
        def _(g):
            pieces(g, lambda i: arrive(2, i))
            send(core_mid, g, block(g)).start()
            accumulate(0, 2, g)

        finish(0, 2)

    @pl.loop(0, groups)
    def _(g):
        arrive(mid_slot, g, block(g))

    meta_arrive(mid_slot)
    acc[0] = product(mid_slot, everything)
    finish(0, mid_slot)

    meta_arrive(far_slot)
    meta_arrive(near_slot)

    @pl.when(role == 0)
    def _():
        send_meta(core_far).start()
        send_meta(core_near).start()

    @pl.when(role == 1)
    def _():
        def step(i):
            arrive(z_slot, i)
            send(relay, i).start()

        pieces(groups - 1, step)
        accumulate(2, z_slot, groups - 1)
        finish(2, z_slot)

    corner = me < 2
    early_slot = jnp.where(corner, near_slot, far_slot)
    late_slot = jnp.where(corner, far_slot, near_slot)
    core_early = tuple(
        jnp.where(corner, a, b) for a, b in zip(core_near, core_far, strict=True)
    )
    core_late = tuple(
        jnp.where(corner, b, a) for a, b in zip(core_near, core_far, strict=True)
    )

    @pl.loop(0, groups - 1)
    def _(g):
        @pl.when(role == 0)
        def _():
            pieces(g, lambda i: arrive(z_slot, i))
            accumulate(2, z_slot, g)
            pieces(g, lambda i: arrive(early_slot, i))
            send(core_early, g * group, block(g)).start()
            pieces(g, lambda i: arrive(late_slot, i))
            send(core_late, g * group, block(g)).start()

        @pl.when(role == 1)
        def _():
            arrive(early_slot, g * group, block(g))
            arrive(late_slot, g * group, block(g))

        accumulate(0, early_slot, g)
        accumulate(1, late_slot, g)

    final = groups - 1

    @pl.when(role == 0)
    def _():
        pieces(final, lambda i: arrive(z_slot, i))
        accumulate(2, z_slot, final)
        finish(2, z_slot)

        def step(i):
            arrive(early_slot, i)
            send(core_early, i).start()

        pieces(final, step)

    @pl.when(role == 1)
    def _():
        pieces(final, lambda i: arrive(early_slot, i))

    accumulate(0, early_slot, final)
    finish(0, early_slot)

    def step(i):
        arrive(late_slot, i)

        @pl.when(role == 0)
        def _():
            send(core_late, i).start()

        acc[1] += product(late_slot, chunk(i))

    pieces(final, step)
    finish(1, late_slot)

    @pl.when(core == 1)
    def _():
        pl.semaphore_wait(gate.at[2], n_dict - 1)
        pl.semaphore_signal(gate.at[2], inc=1, device_id=scan_device(partner))

    @pl.when(core == 0)
    def _():
        pl.semaphore_wait(gate.at[2], 1)

    sums[my_dict] = totals[...]

    def send_sum(d):
        return pltpu.make_async_remote_copy(
            src_ref=totals,
            dst_ref=sums.at[my_dict],
            send_sem=sum_ssem.at[d],
            recv_sem=sum_rsem.at[my_dict],
            device_id={"dict": lax.rem(my_dict + d, n_dict)},
        )

    for d in range(1, n_dict):
        send_sum(d).start()

    for flow in (x_own, z_own, core_own, relay, core_mid):
        sent(flow)
        send_meta(flow).wait_send()

    @pl.when(role == 0)
    def _():
        for flow in (core_far, core_near):
            sent(flow)
            send_meta(flow).wait_send()

    for d in range(1, n_dict):
        source = lax.rem(my_dict + d, n_dict)
        pltpu.make_async_copy(totals, sums.at[source], sum_rsem.at[source]).wait()
    whole = sums[0]
    for d in range(1, n_dict):
        whole = whole + sums[d]
    denominator = whole[7:8]
    quat_out[...] = whole[0:4] / denominator
    prob_out[...] = whole[4:7] / denominator
    for d in range(1, n_dict):
        send_sum(d).wait_send()


def solution(mesh):
    n = mesh.shape["scan"]
    n_dict = mesh.shape["dict"]

    def per_device(patterns, dictionary, orientation_quats, phase_id, valid_count):
        pixels, slots = dictionary.shape
        count = patterns.shape[1]
        chunks = chunk_count(pixels)
        vmem = pl.BlockSpec(memory_space=pltpu.VMEM)
        hbm = pl.BlockSpec(memory_space=pltpu.HBM)
        return pl.pallas_call(
            functools.partial(kernel, n, n_dict, chunks, 3 if chunks % 3 == 0 else 1),
            out_shape=(
                jax.ShapeDtypeStruct((4, count), jnp.float32),
                jax.ShapeDtypeStruct((3, count), jnp.float32),
            ),
            in_specs=[hbm] * 5,
            out_specs=(vmem, vmem),
            scratch_shapes=[
                pltpu.VMEM((SLOTS, pixels, slots), jnp.bfloat16),
                pltpu.VMEM((pixels, count), jnp.bfloat16),
                pltpu.VMEM((SLOTS, 8, slots), jnp.float32),
                pltpu.VMEM((3, slots, count), jnp.float32),
                pltpu.VMEM((n_dict, 8, count), jnp.float32),
                pltpu.VMEM((8, count), jnp.float32),
                pltpu.VMEM((4, slots), jnp.bfloat16),
                pltpu.VMEM((1, slots), jnp.int32),
                pltpu.SMEM((1, 1), jnp.int32),
                pltpu.SemaphoreType.REGULAR((3,)),
                pltpu.SemaphoreType.DMA((7,)),
                pltpu.SemaphoreType.DMA((SLOTS, chunks)),
                pltpu.SemaphoreType.DMA((7,)),
                pltpu.SemaphoreType.DMA((SLOTS,)),
                pltpu.SemaphoreType.DMA((3,)),
                pltpu.SemaphoreType.DMA((5,)),
                pltpu.SemaphoreType.DMA((5,)),
                pltpu.SemaphoreType.DMA((n_dict,)),
                pltpu.SemaphoreType.DMA((n_dict,)),
            ],
            compiler_params=pltpu.CompilerParams(
                collective_id=0, has_side_effects=True, vmem_limit_bytes=62 * 2**20
            ),
        )(dictionary, patterns, orientation_quats, phase_id.reshape(1, slots), valid_count.reshape(1, 1))

    in_specs = (
        P(None, "scan"),
        P(None, ("scan", "dict")),
        P(None, ("scan", "dict")),
        P(("scan", "dict")),
        P(("scan", "dict")),
    )
    out_specs = (P(None, "scan"), P(None, "scan"))
    return jax.shard_map(
        per_device, mesh=mesh, in_specs=in_specs, out_specs=out_specs, check_vma=False
    )
```

```python
import functools

import jax
import jax.numpy as jnp
from jax import lax
from jax.experimental import pallas as pl
from jax.experimental.pallas import tpu as pltpu
from jax.sharding import PartitionSpec as P

REACH = 3
SLOTS = 2 * REACH + 1
EPS = 1e-05
SHARPNESS = 40.0
LAYER = 4


def chunk_count(pixels):
    for count in (15, 9, 5, 3, 25, 16, 8, 4, 2):
        if pixels % (16 * count) == 0:
            return count
    return 1


def kernel(
    n, n_dict, chunks, group, tile_ref, pats_ref, quats_ref, phase_ref, valid_ref,
    whole_out,
    buf, pats, meta, acc, sums, totals, quats, phase, valid,
    gate, ssem, rsem, meta_ssem, meta_rsem, load_sem, tile_sem, pats_sem, sum_ssem, sum_rsem,
):
    pixels, slots = tile_ref.shape
    rows = pixels // chunks
    own = REACH
    me = lax.axis_index("scan")
    my_dict = lax.axis_index("dict")
    j = lax.rem(me, LAYER)
    sign = jnp.where(j < 2, 1, -1)
    role = jnp.where((j == 0) | (j == LAYER - 1), 0, 1)
    rho = 1 - 2 * role

    def at(offset):
        return lax.rem(me + offset + n, n)

    def chunk(i):
        return pl.ds(pl.multiple_of(i * rows, 16), rows)

    core = lax.rem(me, 2)
    partner = rho * sign
    across = 2 * sign
    beyond = -3 * partner

    def scan_device(offset):
        return {"scan": at(offset)}

    def dict_device(d):
        return {"dict": lax.rem(my_dict + d, n_dict)}

    splits = 5

    def piece_of(i):
        size = pixels // splits
        return pl.ds(pl.multiple_of(i * size, 16), size)

    def load_tile(i):
        return pltpu.make_async_copy(
            tile_ref.at[piece_of(i)], buf.at[own, piece_of(i)], tile_sem.at[i]
        )

    def load_pats(i):
        return pltpu.make_async_copy(
            pats_ref.at[piece_of(i)], pats.at[piece_of(i)], pats_sem.at[i]
        )

    @pl.loop(0, splits)
    def _(i):
        load_tile(i).start()

    loads = [
        pltpu.make_async_copy(src, dst, load_sem.at[k])
        for k, (src, dst) in enumerate(
            ((quats_ref, quats), (phase_ref, phase), (valid_ref, valid))
        )
    ]
    for load in loads:
        load.start()

    barrier = pltpu.get_barrier_semaphore()
    pl.semaphore_signal(barrier, inc=1, device_id=scan_device(partner))
    pl.semaphore_signal(barrier, inc=1, device_id=scan_device(beyond))

    @pl.when(core == 1)
    def _():
        pl.semaphore_signal(barrier, inc=1, device_id=scan_device(across))
        for d in range(1, n_dict):
            pl.semaphore_signal(barrier, inc=1, device_id=dict_device(d))


    def column_stats(ref, lanes, load):
        width = ref.shape[-1]
        size = pixels // splits
        load(0).wait()
        shift = ref[pl.ds(0, 1), :].astype(jnp.float32)

        def piece(i, carry):
            @pl.when(i > 0)
            def _():
                load(i).wait()

            def step(k, carry):
                first, second = carry
                start = pl.multiple_of(i * size + k * lanes * 3, 16)
                x = ref[pl.ds(start, lanes * 3), :].astype(jnp.float32) - shift
                first = first + jnp.sum(x.reshape(3, lanes, width), axis=0)
                second = second + jnp.sum((x * x).reshape(3, lanes, width), axis=0)
                return first, second

            return lax.fori_loop(0, size // (lanes * 3), step, carry)

        zero = jnp.zeros((lanes, width), jnp.float32)
        first, second = lax.fori_loop(0, splits, piece, (zero, zero))
        first = jnp.sum(first, axis=0, keepdims=True) / pixels
        second = jnp.sum(second, axis=0, keepdims=True) / pixels
        return first + shift, lax.rsqrt((second - first * first + EPS) * pixels)

    @pl.when(core == 0)
    def _():
        pl.semaphore_wait(barrier, 2)

    @pl.when(core == 1)
    def _():
        pl.semaphore_wait(barrier, 2 + n_dict)

    core_own = (0, None, partner, -rho)
    x_own = (1, None, across, 2)
    z_own = (2, None, beyond, 3 * rho)
    relay = (3, 2 + role, (4 - 2 * role) * sign, role - 2)
    core_mid = (4, 2, partner, 2 - rho)
    core_far = (5, -2, partner, -3)
    core_near = (6, -1, partner, -2)

    def send(flow, i, part=None):
        number, source, offset, slot = flow
        part = chunk(i) if part is None else part
        return pltpu.make_async_remote_copy(
            src_ref=tile_ref.at[part] if source is None else buf.at[source + own, part],
            dst_ref=buf.at[slot + own, part],
            send_sem=ssem.at[number],
            recv_sem=rsem.at[slot + own, i],
            device_id={"scan": at(offset)},
        )

    def sent(flow):
        pltpu.make_async_copy(tile_ref, buf.at[own], ssem.at[flow[0]]).wait()

    def arrive(slot, i, part=None):
        part = chunk(i) if part is None else part
        pltpu.make_async_copy(
            tile_ref.at[part], buf.at[slot + own, part], rsem.at[slot + own, i]
        ).wait()

    everything = pl.ds(0, pixels)

    def block(g):
        return pl.ds(pl.multiple_of(g * (group * rows), 16), group * rows)

    def send_meta(flow):
        number, source, offset, slot = flow
        return pltpu.make_async_remote_copy(
            src_ref=meta.at[own if source is None else source + own],
            dst_ref=meta.at[slot + own],
            send_sem=meta_ssem.at[number],
            recv_sem=meta_rsem.at[slot + own],
            device_id={"scan": at(offset)},
        )

    def meta_arrive(slot):
        pltpu.make_async_copy(
            meta.at[own], meta.at[slot + own], meta_rsem.at[slot + own]
        ).wait()

    edge = jnp.where(role == 0, jnp.where(j == 0, me + LAYER >= n, me < LAYER), False)
    last = chunks - jnp.where(edge, group, 0)
    ahead = chunks // 3

    pl.semaphore_signal(gate.at[0], inc=1, device_id=scan_device(partner))

    @pl.when(core == 1)
    def _():
        pl.semaphore_signal(gate.at[1], inc=1, device_id=scan_device(across))
        for d in range(1, n_dict):
            pl.semaphore_signal(gate.at[2], inc=1, device_id=dict_device(d))

    def send_own(i, lanes):
        @pl.when(i < last)
        def _():
            send(z_own, i).start()

        if lanes:
            send(x_own, i).start()

    begin = chunks // 3

    @pl.when(core == 1)
    def _():
        @pl.loop(0, begin)
        def _(i):
            send_own(i, True)

        pl.semaphore_wait(gate.at[1], 1)
        pl.semaphore_signal(gate.at[1], inc=1, device_id=scan_device(partner))

    @pl.when(core == 0)
    def _():
        @pl.loop(0, begin)
        def _(i):
            send_own(i, False)

        pl.semaphore_wait(gate.at[1], 1)

        @pl.loop(0, begin)
        def _(i):
            send(x_own, i).start()

    mean, scale = column_stats(buf.at[own], 48, load_tile)

    @pl.loop(0, splits)
    def _(i):
        load_pats(i).start()

    for load in loads:
        load.wait()

    live = (
        lax.broadcasted_iota(jnp.int32, (1, slots), 1) < valid[0, 0]
    ).astype(jnp.float32)
    meta[own, 0:4, :] = quats[...].astype(jnp.float32) * live
    for p in range(3):
        meta[own, 4 + p : 5 + p, :] = (phase[...] == p).astype(jnp.float32) * live
    meta[own, 7:8, :] = live
    meta[own, 8:9, :] = mean
    meta[own, 9:10, :] = scale
    meta[own, 10:16, :] = jnp.zeros((6, slots), jnp.float32)
    send_meta(z_own).start()
    send_meta(x_own).start()

    @pl.loop(begin, chunks)
    def _(i):
        send_own(i, True)

    pl.semaphore_wait(gate.at[0], 1)
    send(core_own, 0, everything).start()

    send_meta(core_own).start()

    p_mean, p_scale = column_stats(pats, 16, load_pats)

    @pl.loop(0, 25)
    def _(i):
        size = pixels // 25
        part = pl.ds(pl.multiple_of(i * size, 16), size)
        pats[part, :] = ((pats[part, :].astype(jnp.float32) - p_mean) * p_scale).astype(
            jnp.bfloat16
        )

    totals[...] = jnp.zeros_like(totals)

    def product(slot, part):
        raw = buf[slot + own, part, :].astype(jnp.float32)
        unit = (raw - meta[slot + own, 8:9, :]) * meta[slot + own, 9:10, :]
        return lax.dot_general(
            unit.astype(jnp.bfloat16), pats[part, :], (((0,), (0,)), ((), ())),
            preferred_element_type=jnp.float32,
        )

    def accumulate(which, slot, g):
        if isinstance(g, int):
            acc[which] += product(slot, block(g))
            return

        @pl.when(g == 0)
        def _():
            acc[which] = product(slot, block(g))

        @pl.when(g > 0)
        def _():
            acc[which] += product(slot, block(g))

    def finish(which, slot):
        weights = jnp.exp(SHARPNESS * (acc[which] - 1.0)).astype(jnp.bfloat16)
        table = meta[slot + own, 0:8, :].astype(jnp.bfloat16)
        totals[...] += jnp.dot(table, weights, preferred_element_type=jnp.float32)

    acc[0] = product(0, everything)
    finish(0, 0)
    arrive(rho, 0, everything)
    meta_arrive(rho)
    acc[1] = product(rho, everything)
    finish(1, rho)

    z_slot = -3 * rho
    mid_slot = 2 + rho
    far_slot = -2 - role
    near_slot = -1 - role
    groups = chunks // group

    def pieces(g, body):
        @pl.loop(0, group)
        def _(c):
            body(g * group + c)

    @pl.when(role == 0)
    def _():
        meta_arrive(2)
        send_meta(relay).start()
        send_meta(core_mid).start()

        @pl.loop(0, groups)
        def _(g):
            def step(i):
                arrive(2, i)
                send(relay, i).start()

                @pl.when((i >= ahead) & (last + i - ahead < chunks))
                def _():
                    send(z_own, last + i - ahead).start()

            pieces(g, step)
            send(core_mid, g, block(g)).start()
            accumulate(0, 2, g)

        finish(0, 2)
        meta_arrive(z_slot)

    @pl.when(role == 1)
    def _():
        meta_arrive(z_slot)
        send_meta(relay).start()

        @pl.loop(0, groups - 1)
        def _(g):
            def step(i):
                arrive(z_slot, i)
                send(relay, i).start()

            pieces(g, step)
            accumulate(2, z_slot, g)

        meta_arrive(2)
        send_meta(core_mid).start()

        @pl.loop(0, groups)
        def _(g):
            pieces(g, lambda i: arrive(2, i))
            send(core_mid, g, block(g)).start()
            accumulate(0, 2, g)

        finish(0, 2)

    @pl.loop(0, groups)
    def _(g):
        arrive(mid_slot, g, block(g))

    meta_arrive(mid_slot)
    acc[0] = product(mid_slot, everything)
    finish(0, mid_slot)

    meta_arrive(far_slot)
    meta_arrive(near_slot)

    @pl.when(role == 0)
    def _():
        send_meta(core_far).start()
        send_meta(core_near).start()

    @pl.when(role == 1)
    def _():
        def step(i):
            arrive(z_slot, i)
            send(relay, i).start()

        pieces(groups - 1, step)
        accumulate(2, z_slot, groups - 1)
        finish(2, z_slot)

    corner = me < 2
    early_slot = jnp.where(corner, near_slot, far_slot)
    late_slot = jnp.where(corner, far_slot, near_slot)
    core_early = tuple(
        jnp.where(corner, a, b) for a, b in zip(core_near, core_far, strict=True)
    )
    core_late = tuple(
        jnp.where(corner, b, a) for a, b in zip(core_near, core_far, strict=True)
    )

    @pl.loop(0, groups - 1)
    def _(g):
        @pl.when(role == 0)
        def _():
            pieces(g, lambda i: arrive(z_slot, i))
            accumulate(2, z_slot, g)
            pieces(g, lambda i: arrive(early_slot, i))
            send(core_early, g * group, block(g)).start()
            pieces(g, lambda i: arrive(late_slot, i))
            send(core_late, g * group, block(g)).start()

        @pl.when(role == 1)
        def _():
            arrive(early_slot, g * group, block(g))
            arrive(late_slot, g * group, block(g))

        accumulate(0, early_slot, g)
        accumulate(1, late_slot, g)

    final = groups - 1

    @pl.when(role == 0)
    def _():
        pieces(final, lambda i: arrive(z_slot, i))
        accumulate(2, z_slot, final)
        finish(2, z_slot)

        def step(i):
            arrive(early_slot, i)
            send(core_early, i).start()

        pieces(final, step)

    @pl.when(role == 1)
    def _():
        pieces(final, lambda i: arrive(early_slot, i))

    accumulate(0, early_slot, final)
    finish(0, early_slot)

    def step(i):
        arrive(late_slot, i)

        @pl.when(role == 0)
        def _():
            send(core_late, i).start()

        acc[1] += product(late_slot, chunk(i))

    pieces(final, step)
    finish(1, late_slot)

    @pl.when(core == 1)
    def _():
        pl.semaphore_wait(gate.at[2], n_dict - 1)
        pl.semaphore_signal(gate.at[2], inc=1, device_id=scan_device(partner))

    @pl.when(core == 0)
    def _():
        pl.semaphore_wait(gate.at[2], 1)

    sums[my_dict] = totals[...]

    def send_sum(d):
        return pltpu.make_async_remote_copy(
            src_ref=totals,
            dst_ref=sums.at[my_dict],
            send_sem=sum_ssem.at[d],
            recv_sem=sum_rsem.at[my_dict],
            device_id={"dict": lax.rem(my_dict + d, n_dict)},
        )

    for d in range(1, n_dict):
        send_sum(d).start()

    for flow in (x_own, z_own, core_own, relay, core_mid):
        sent(flow)
        send_meta(flow).wait_send()

    @pl.when(role == 0)
    def _():
        for flow in (core_far, core_near):
            sent(flow)
            send_meta(flow).wait_send()

    for d in range(1, n_dict):
        source = lax.rem(my_dict + d, n_dict)
        pltpu.make_async_copy(totals, sums.at[source], sum_rsem.at[source]).wait()
    whole = sums[0]
    for d in range(1, n_dict):
        whole = whole + sums[d]
    whole_out[...] = whole
    for d in range(1, n_dict):
        send_sum(d).wait_send()


def divide(whole_ref, quat_out, prob_out):
    denominator = whole_ref[7:8, :]
    quat_out[...] = whole_ref[0:4, :] / denominator
    prob_out[...] = whole_ref[4:7, :] / denominator


def solution(mesh):
    n = mesh.shape["scan"]
    n_dict = mesh.shape["dict"]

    def per_device(patterns, dictionary, orientation_quats, phase_id, valid_count):
        pixels, slots = dictionary.shape
        count = patterns.shape[1]
        chunks = chunk_count(pixels)
        vmem = pl.BlockSpec(memory_space=pltpu.VMEM)
        hbm = pl.BlockSpec(memory_space=pltpu.HBM)
        whole = pl.pallas_call(
            functools.partial(kernel, n, n_dict, chunks, 3 if chunks % 3 == 0 else 1),
            out_shape=jax.ShapeDtypeStruct((8, count), jnp.float32),
            in_specs=[hbm] * 5,
            out_specs=vmem,
            scratch_shapes=[
                pltpu.VMEM((SLOTS, pixels, slots), jnp.bfloat16),
                pltpu.VMEM((pixels, count), jnp.bfloat16),
                pltpu.VMEM((SLOTS, 16, slots), jnp.float32),
                pltpu.VMEM((3, slots, count), jnp.float32),
                pltpu.VMEM((n_dict, 8, count), jnp.float32),
                pltpu.VMEM((8, count), jnp.float32),
                pltpu.VMEM((4, slots), jnp.bfloat16),
                pltpu.VMEM((1, slots), jnp.int32),
                pltpu.SMEM((1, 1), jnp.int32),
                pltpu.SemaphoreType.REGULAR((3,)),
                pltpu.SemaphoreType.DMA((7,)),
                pltpu.SemaphoreType.DMA((SLOTS, chunks)),
                pltpu.SemaphoreType.DMA((7,)),
                pltpu.SemaphoreType.DMA((SLOTS,)),
                pltpu.SemaphoreType.DMA((3,)),
                pltpu.SemaphoreType.DMA((5,)),
                pltpu.SemaphoreType.DMA((5,)),
                pltpu.SemaphoreType.DMA((n_dict,)),
                pltpu.SemaphoreType.DMA((n_dict,)),
            ],
            compiler_params=pltpu.CompilerParams(
                collective_id=0, has_side_effects=True, vmem_limit_bytes=62 * 2**20
            ),
        )(dictionary, patterns, orientation_quats, phase_id.reshape(1, slots), valid_count.reshape(1, 1))

        return pl.pallas_call(
            divide,
            out_shape=(
                jax.ShapeDtypeStruct((4, count), jnp.float32),
                jax.ShapeDtypeStruct((3, count), jnp.float32),
            ),
            in_specs=[vmem],
            out_specs=(vmem, vmem),
        )(whole)

    in_specs = (
        P(None, "scan"),
        P(None, ("scan", "dict")),
        P(None, ("scan", "dict")),
        P(("scan", "dict")),
        P(("scan", "dict")),
    )
    out_specs = (P(None, "scan"), P(None, "scan"))
    return jax.shard_map(
        per_device, mesh=mesh, in_specs=in_specs, out_specs=out_specs, check_vma=False
    )
```

```python
import functools

import jax
import jax.numpy as jnp
from jax import lax
from jax.experimental import pallas as pl
from jax.experimental.pallas import tpu as pltpu
from jax.sharding import PartitionSpec as P

REACH = 3
SLOTS = 2 * REACH + 1
EPS = 1e-05
SHARPNESS = 40.0
LAYER = 4


def chunk_count(pixels):
    for count in (15, 9, 5, 3, 25, 16, 8, 4, 2):
        if pixels % (16 * count) == 0:
            return count
    return 1


def kernel(
    n, n_dict, chunks, group, tile_ref, pats_ref, quats_ref, phase_ref, valid_ref,
    whole_out,
    buf, pats, meta, acc, sums, totals, quats, phase, valid,
    gate, ssem, rsem, meta_ssem, meta_rsem, load_sem, tile_sem, pats_sem, sum_ssem, sum_rsem,
):
    pixels, slots = tile_ref.shape
    rows = pixels // chunks
    own = REACH
    me = lax.axis_index("scan")
    my_dict = lax.axis_index("dict")
    j = lax.rem(me, LAYER)
    sign = jnp.where(j < 2, 1, -1)
    role = jnp.where((j == 0) | (j == LAYER - 1), 0, 1)
    rho = 1 - 2 * role

    def at(offset):
        return lax.rem(me + offset + n, n)

    def chunk(i):
        return pl.ds(pl.multiple_of(i * rows, 16), rows)

    core = lax.rem(me, 2)
    partner = rho * sign
    across = 2 * sign
    beyond = -3 * partner

    def scan_device(offset):
        return {"scan": at(offset)}

    def dict_device(d):
        return {"dict": lax.rem(my_dict + d, n_dict)}

    splits = 5

    def piece_of(i):
        size = pixels // splits
        return pl.ds(pl.multiple_of(i * size, 16), size)

    def load_tile(i):
        return pltpu.make_async_copy(
            tile_ref.at[piece_of(i)], buf.at[own, piece_of(i)], tile_sem.at[i]
        )

    def load_pats(i):
        return pltpu.make_async_copy(
            pats_ref.at[piece_of(i)], pats.at[piece_of(i)], pats_sem.at[i]
        )

    @pl.loop(0, splits)
    def _(i):
        load_tile(i).start()

    loads = [
        pltpu.make_async_copy(src, dst, load_sem.at[k])
        for k, (src, dst) in enumerate(
            ((quats_ref, quats), (phase_ref, phase), (valid_ref, valid))
        )
    ]
    for load in loads:
        load.start()

    barrier = pltpu.get_barrier_semaphore()
    pl.semaphore_signal(barrier, inc=1, device_id=scan_device(partner))
    pl.semaphore_signal(barrier, inc=1, device_id=scan_device(beyond))

    @pl.when(core == 1)
    def _():
        pl.semaphore_signal(barrier, inc=1, device_id=scan_device(across))
        for d in range(1, n_dict):
            pl.semaphore_signal(barrier, inc=1, device_id=dict_device(d))


    def column_stats(ref, lanes, load):
        width = ref.shape[-1]
        size = pixels // splits
        load(0).wait()
        shift = ref[pl.ds(0, 1), :].astype(jnp.float32)

        def piece(i, carry):
            @pl.when(i > 0)
            def _():
                load(i).wait()

            def step(k, carry):
                first, second = carry
                start = pl.multiple_of(i * size + k * lanes * 3, 16)
                x = ref[pl.ds(start, lanes * 3), :].astype(jnp.float32) - shift
                first = first + jnp.sum(x.reshape(3, lanes, width), axis=0)
                second = second + jnp.sum((x * x).reshape(3, lanes, width), axis=0)
                return first, second

            return lax.fori_loop(0, size // (lanes * 3), step, carry)

        zero = jnp.zeros((lanes, width), jnp.float32)
        first, second = lax.fori_loop(0, splits, piece, (zero, zero))
        first = jnp.sum(first, axis=0, keepdims=True) / pixels
        second = jnp.sum(second, axis=0, keepdims=True) / pixels
        return first + shift, lax.rsqrt((second - first * first + EPS) * pixels)

    @pl.when(core == 0)
    def _():
        pl.semaphore_wait(barrier, 2)

    @pl.when(core == 1)
    def _():
        pl.semaphore_wait(barrier, 2 + n_dict)

    core_own = (0, None, partner, -rho)
    x_own = (1, None, across, 2)
    z_own = (2, None, beyond, 3 * rho)
    relay = (3, 2 + role, (4 - 2 * role) * sign, role - 2)
    core_mid = (4, 2, partner, 2 - rho)
    core_far = (5, -2, partner, -3)
    core_near = (6, -1, partner, -2)

    def send(flow, i, part=None):
        number, source, offset, slot = flow
        part = chunk(i) if part is None else part
        return pltpu.make_async_remote_copy(
            src_ref=tile_ref.at[part] if source is None else buf.at[source + own, part],
            dst_ref=buf.at[slot + own, part],
            send_sem=ssem.at[number],
            recv_sem=rsem.at[slot + own, i],
            device_id={"scan": at(offset)},
        )

    def sent(flow):
        pltpu.make_async_copy(tile_ref, buf.at[own], ssem.at[flow[0]]).wait()

    def arrive(slot, i, part=None):
        part = chunk(i) if part is None else part
        pltpu.make_async_copy(
            tile_ref.at[part], buf.at[slot + own, part], rsem.at[slot + own, i]
        ).wait()

    everything = pl.ds(0, pixels)

    def block(g):
        return pl.ds(pl.multiple_of(g * (group * rows), 16), group * rows)

    def send_meta(flow):
        number, source, offset, slot = flow
        return pltpu.make_async_remote_copy(
            src_ref=meta.at[own if source is None else source + own],
            dst_ref=meta.at[slot + own],
            send_sem=meta_ssem.at[number],
            recv_sem=meta_rsem.at[slot + own],
            device_id={"scan": at(offset)},
        )

    def meta_arrive(slot):
        pltpu.make_async_copy(
            meta.at[own], meta.at[slot + own], meta_rsem.at[slot + own]
        ).wait()

    edge = jnp.where(role == 0, jnp.where(j == 0, me + LAYER >= n, me < LAYER), False)
    last = chunks - jnp.where(edge, group, 0)
    ahead = 3

    pl.semaphore_signal(gate.at[0], inc=1, device_id=scan_device(partner))

    @pl.when(core == 1)
    def _():
        pl.semaphore_signal(gate.at[1], inc=1, device_id=scan_device(across))
        for d in range(1, n_dict):
            pl.semaphore_signal(gate.at[2], inc=1, device_id=dict_device(d))

    def send_own(i, lanes):
        @pl.when(i < last)
        def _():
            send(z_own, i).start()

        if lanes:
            send(x_own, i).start()

    begin = 3

    @pl.when(core == 1)
    def _():
        @pl.loop(0, begin)
        def _(i):
            send_own(i, True)

        pl.semaphore_wait(gate.at[1], 1)
        pl.semaphore_signal(gate.at[1], inc=1, device_id=scan_device(partner))

    @pl.when(core == 0)
    def _():
        @pl.loop(0, begin)
        def _(i):
            send_own(i, False)

        pl.semaphore_wait(gate.at[1], 1)

        @pl.loop(0, begin)
        def _(i):
            send(x_own, i).start()

    mean, scale = column_stats(buf.at[own], 48, load_tile)

    @pl.loop(0, splits)
    def _(i):
        load_pats(i).start()

    for load in loads:
        load.wait()

    live = (
        lax.broadcasted_iota(jnp.int32, (1, slots), 1) < valid[0, 0]
    ).astype(jnp.float32)
    meta[own, 0:4, :] = quats[...].astype(jnp.float32) * live
    for p in range(3):
        meta[own, 4 + p : 5 + p, :] = (phase[...] == p).astype(jnp.float32) * live
    meta[own, 7:8, :] = live
    meta[own, 8:9, :] = mean
    meta[own, 9:10, :] = scale
    meta[own, 10:16, :] = jnp.zeros((6, slots), jnp.float32)
    send_meta(z_own).start()
    send_meta(x_own).start()

    @pl.loop(begin, chunks)
    def _(i):
        send_own(i, True)

    pl.semaphore_wait(gate.at[0], 1)
    send(core_own, 0, everything).start()

    send_meta(core_own).start()

    p_mean, p_scale = column_stats(pats, 16, load_pats)

    @pl.loop(0, 25)
    def _(i):
        size = pixels // 25
        part = pl.ds(pl.multiple_of(i * size, 16), size)
        pats[part, :] = ((pats[part, :].astype(jnp.float32) - p_mean) * p_scale).astype(
            jnp.bfloat16
        )

    totals[...] = jnp.zeros_like(totals)

    def product(slot, part):
        raw = buf[slot + own, part, :].astype(jnp.float32)
        unit = (raw - meta[slot + own, 8:9, :]) * meta[slot + own, 9:10, :]
        return lax.dot_general(
            unit.astype(jnp.bfloat16), pats[part, :], (((0,), (0,)), ((), ())),
            preferred_element_type=jnp.float32,
        )

    def accumulate(which, slot, g):
        if isinstance(g, int):
            acc[which] += product(slot, block(g))
            return

        @pl.when(g == 0)
        def _():
            acc[which] = product(slot, block(g))

        @pl.when(g > 0)
        def _():
            acc[which] += product(slot, block(g))

    def finish(which, slot, part=None):
        cosine = acc[which]
        if part is not None:
            cosine = cosine + product(slot, part)
        weights = jnp.exp(SHARPNESS * (cosine - 1.0)).astype(jnp.bfloat16)
        table = meta[slot + own, 0:8, :].astype(jnp.bfloat16)
        totals[...] += jnp.dot(table, weights, preferred_element_type=jnp.float32)

    acc[0] = product(0, everything)
    finish(0, 0)
    arrive(rho, 0, everything)
    meta_arrive(rho)
    acc[1] = product(rho, everything)
    finish(1, rho)

    z_slot = -3 * rho
    mid_slot = 2 + rho
    far_slot = -2 - role
    near_slot = -1 - role
    groups = chunks // group

    def pieces(g, body):
        @pl.loop(0, group)
        def _(c):
            body(g * group + c)

    @pl.when(role == 0)
    def _():
        meta_arrive(2)
        send_meta(relay).start()
        send_meta(core_mid).start()

        @pl.loop(0, groups)
        def _(g):
            def step(i):
                arrive(2, i)
                send(relay, i).start()

                @pl.when((i >= ahead) & (last + i - ahead < chunks))
                def _():
                    send(z_own, last + i - ahead).start()

            pieces(g, step)
            send(core_mid, g, block(g)).start()
            accumulate(0, 2, g)

        finish(0, 2)
        meta_arrive(z_slot)

    @pl.when(role == 1)
    def _():
        meta_arrive(z_slot)
        send_meta(relay).start()

        @pl.loop(0, groups - 1)
        def _(g):
            def step(i):
                arrive(z_slot, i)
                send(relay, i).start()

            pieces(g, step)
            accumulate(2, z_slot, g)

        meta_arrive(2)
        send_meta(core_mid).start()

        @pl.loop(0, groups)
        def _(g):
            pieces(g, lambda i: arrive(2, i))
            send(core_mid, g, block(g)).start()
            accumulate(0, 2, g)

        finish(0, 2)

    @pl.loop(0, groups)
    def _(g):
        arrive(mid_slot, g, block(g))

    meta_arrive(mid_slot)
    acc[0] = product(mid_slot, everything)
    finish(0, mid_slot)

    meta_arrive(far_slot)
    meta_arrive(near_slot)

    @pl.when(role == 0)
    def _():
        send_meta(core_far).start()
        send_meta(core_near).start()

    @pl.when(role == 1)
    def _():
        def step(i):
            arrive(z_slot, i)
            send(relay, i).start()

        pieces(groups - 1, step)
        accumulate(2, z_slot, groups - 1)
        finish(2, z_slot)

    corner = me < 2
    early_slot = jnp.where(corner, near_slot, far_slot)
    late_slot = jnp.where(corner, far_slot, near_slot)
    core_early = tuple(
        jnp.where(corner, a, b) for a, b in zip(core_near, core_far, strict=True)
    )
    core_late = tuple(
        jnp.where(corner, b, a) for a, b in zip(core_near, core_far, strict=True)
    )

    @pl.loop(0, groups - 1)
    def _(g):
        @pl.when(role == 0)
        def _():
            pieces(g, lambda i: arrive(z_slot, i))
            accumulate(2, z_slot, g)
            pieces(g, lambda i: arrive(early_slot, i))
            send(core_early, g * group, block(g)).start()
            pieces(g, lambda i: arrive(late_slot, i))
            send(core_late, g * group, block(g)).start()

        @pl.when(role == 1)
        def _():
            arrive(early_slot, g * group, block(g))
            arrive(late_slot, g * group, block(g))

        accumulate(0, early_slot, g)
        accumulate(1, late_slot, g)

    final = groups - 1

    @pl.when(role == 0)
    def _():
        pieces(final, lambda i: arrive(z_slot, i))
        accumulate(2, z_slot, final)
        finish(2, z_slot)

        def step(i):
            arrive(early_slot, i)
            send(core_early, i).start()

        pieces(final, step)

    @pl.when(role == 1)
    def _():
        pieces(final, lambda i: arrive(early_slot, i))

    finish(0, early_slot, block(final))

    def arrive_late(i):
        arrive(late_slot, i)

        @pl.when(role == 0)
        def _():
            send(core_late, i).start()

    @pl.loop(chunks - group, chunks - 1)
    def _(i):
        arrive_late(i)
        acc[1] += product(late_slot, chunk(i))

    arrive_late(chunks - 1)
    finish(1, late_slot, chunk(chunks - 1))

    @pl.when(core == 1)
    def _():
        pl.semaphore_wait(gate.at[2], n_dict - 1)
        pl.semaphore_signal(gate.at[2], inc=1, device_id=scan_device(partner))

    @pl.when(core == 0)
    def _():
        pl.semaphore_wait(gate.at[2], 1)

    sums[my_dict] = totals[...]

    def send_sum(d):
        return pltpu.make_async_remote_copy(
            src_ref=totals,
            dst_ref=sums.at[my_dict],
            send_sem=sum_ssem.at[d],
            recv_sem=sum_rsem.at[my_dict],
            device_id={"dict": lax.rem(my_dict + d, n_dict)},
        )

    for d in range(1, n_dict):
        send_sum(d).start()

    for flow in (x_own, z_own, core_own, relay, core_mid):
        sent(flow)
        send_meta(flow).wait_send()

    @pl.when(role == 0)
    def _():
        for flow in (core_far, core_near):
            sent(flow)
            send_meta(flow).wait_send()

    for d in range(1, n_dict):
        source = lax.rem(my_dict + d, n_dict)
        pltpu.make_async_copy(totals, sums.at[source], sum_rsem.at[source]).wait()
    whole = sums[0]
    for d in range(1, n_dict):
        whole = whole + sums[d]
    whole_out[...] = whole
    for d in range(1, n_dict):
        send_sum(d).wait_send()


def divide(whole_ref, quat_out, prob_out):
    denominator = whole_ref[7:8, :]
    quat_out[...] = whole_ref[0:4, :] / denominator
    prob_out[...] = whole_ref[4:7, :] / denominator


def solution(mesh):
    n = mesh.shape["scan"]
    n_dict = mesh.shape["dict"]

    def per_device(patterns, dictionary, orientation_quats, phase_id, valid_count):
        pixels, slots = dictionary.shape
        count = patterns.shape[1]
        chunks = chunk_count(pixels)
        vmem = pl.BlockSpec(memory_space=pltpu.VMEM)
        hbm = pl.BlockSpec(memory_space=pltpu.HBM)
        whole = pl.pallas_call(
            functools.partial(kernel, n, n_dict, chunks, 3 if chunks % 3 == 0 else 1),
            out_shape=jax.ShapeDtypeStruct((8, count), jnp.float32),
            in_specs=[hbm] * 5,
            out_specs=vmem,
            scratch_shapes=[
                pltpu.VMEM((SLOTS, pixels, slots), jnp.bfloat16),
                pltpu.VMEM((pixels, count), jnp.bfloat16),
                pltpu.VMEM((SLOTS, 16, slots), jnp.float32),
                pltpu.VMEM((3, slots, count), jnp.float32),
                pltpu.VMEM((n_dict, 8, count), jnp.float32),
                pltpu.VMEM((8, count), jnp.float32),
                pltpu.VMEM((4, slots), jnp.bfloat16),
                pltpu.VMEM((1, slots), jnp.int32),
                pltpu.SMEM((1, 1), jnp.int32),
                pltpu.SemaphoreType.REGULAR((3,)),
                pltpu.SemaphoreType.DMA((7,)),
                pltpu.SemaphoreType.DMA((SLOTS, chunks)),
                pltpu.SemaphoreType.DMA((7,)),
                pltpu.SemaphoreType.DMA((SLOTS,)),
                pltpu.SemaphoreType.DMA((3,)),
                pltpu.SemaphoreType.DMA((5,)),
                pltpu.SemaphoreType.DMA((5,)),
                pltpu.SemaphoreType.DMA((n_dict,)),
                pltpu.SemaphoreType.DMA((n_dict,)),
            ],
            compiler_params=pltpu.CompilerParams(
                collective_id=0, has_side_effects=True, vmem_limit_bytes=62 * 2**20
            ),
        )(dictionary, patterns, orientation_quats, phase_id.reshape(1, slots), valid_count.reshape(1, 1))

        return pl.pallas_call(
            divide,
            out_shape=(
                jax.ShapeDtypeStruct((4, count), jnp.float32),
                jax.ShapeDtypeStruct((3, count), jnp.float32),
            ),
            in_specs=[vmem],
            out_specs=(vmem, vmem),
        )(whole)

    in_specs = (
        P(None, "scan"),
        P(None, ("scan", "dict")),
        P(None, ("scan", "dict")),
        P(("scan", "dict")),
        P(("scan", "dict")),
    )
    out_specs = (P(None, "scan"), P(None, "scan"))
    return jax.shard_map(
        per_device, mesh=mesh, in_specs=in_specs, out_specs=out_specs, check_vma=False
    )
```
